32 devices in a mesh: grp: 2 (over x), kv: 16 (over z, y, core).
Axes of the slice: x: 2, y: 2, z: 4, core: 2. Of those that a mesh axis runs over, the one named last changes fastest.
Arguments:
- absorbed_query: bfloat16 [8, 128, 576], P('grp', 'kv'), parts along dimension 0, may hold values from -65 to 65
- latent_cache: bfloat16 [8, 32768, 576], P('grp', 'kv'), parts along dimension 0, may hold values from -6 to 6
- slot_position: int32 [8, 32768], P('grp', 'kv'), parts along dimension 0, may hold values from 0 to 32767, as said below
- context_lengths: int32 [8], P('grp'), parts along dimension 0, may hold values from 16384 to 32768, as said below
- value_up: bfloat16 [128, 512, 128], P('kv'), may hold values from -2.09375 to 2.09375
Outputs:
- attended: bfloat16 [8, 16384], P('grp', 'kv'), parts along dimension 0
The draws below stay inside these ranges and needn't reach their ends.
There are 2 independent parts, one for each index of `grp`. The reference program is written for one: setup_inputs(seed, part) draws one part's arguments, and reference() takes and returns one part's arrays. A program takes and returns all parts, laid end to end along the dimension named above; an argument that names none is the same for every part. Nothing has to cross between parts.
Inputs may be any that keep to these rules, and one draw needn't show every extreme that they name: `slot_position`: each row is an ordering of 0 to 32767. `context_lengths`: some request holds exactly 32768 tokens.
All inputs are finite; a program needn't handle non-finite values.
Results may differ from the reference program's by a relative error of at most 0.0095.
Values may be sent and summed in bfloat16 or wider, within the bound.
A program may use at most 64 MiB of HBM per device.

```python
import jax
import jax.numpy as jnp
from jax import lax

H = 128
DL = 512
VH = 128
REQ = 4
DQ = 576
SLOTS = 32768


def permuted_rows(key):
    row_keys = jax.random.split(jax.random.fold_in(key, 101), REQ)
    return jax.vmap(lambda row_key: jax.random.permutation(row_key, SLOTS))(row_keys).astype(jnp.int32)


def draw_absorbed_query(key, part):
    drawn = jnp.clip(jax.random.normal(jax.random.fold_in(key, 11), (REQ, H, DQ), jnp.float32), -6.0, 6.0) * 1.3
    return drawn.astype(jnp.bfloat16)


def draw_latent_cache(key, part):
    drawn = jnp.clip(jax.random.normal(jax.random.fold_in(key, 12), (REQ, SLOTS, DQ), jnp.float32), -6.0, 6.0)
    return drawn.astype(jnp.bfloat16)


def draw_slot_position(key, part):
    return permuted_rows(key)


def draw_context_lengths(key, part):
    drawn = jax.random.randint(jax.random.fold_in(key, 13), (REQ,), SLOTS // 2, SLOTS + 1).astype(jnp.int32)
    longest = jax.random.randint(jax.random.fold_in(key, 14), (), 0, REQ).astype(jnp.int32)
    return jnp.where(jnp.arange(REQ, dtype=jnp.int32) == longest, jnp.int32(SLOTS), drawn).astype(jnp.int32)


def block_scale(stream_key, extent, shards, smallest, top_value):
    loudness, own = 1.0, jax.random.fold_in(stream_key, 6)
    for dim, blocks in shards:
        heights = jnp.exp(jax.random.uniform(jax.random.fold_in(own, dim), (blocks,), jnp.float32, smallest / len(shards), top_value / len(shards)))
        loudness = loudness * jnp.repeat(heights, extent[dim] // blocks).reshape([-1 if axis == dim else 1 for axis in range(len(extent))])
    return loudness


def normal_values(stream_key, dims, spread, bound, pieces=(), held_as=jnp.bfloat16):
    entries = spread * jax.random.normal(stream_key, dims, jnp.float32)
    if pieces:
        entries = entries * block_scale(stream_key, dims, pieces, -0.22, 0.18)
    return jnp.clip(entries, -bound, bound).astype(held_as)


def setup_inputs(seed: int = 0, part: int = 0) -> dict:
    splits = jax.random.split(jax.random.key(seed), 6)
    part_splits = jax.random.split(jax.random.fold_in(splits[5], part), 6)
    return {
        "absorbed_query": draw_absorbed_query(jax.random.fold_in(jax.random.fold_in(splits[5], part), 71), part),
        "latent_cache": draw_latent_cache(jax.random.fold_in(jax.random.fold_in(splits[5], part), 71), part),
        "slot_position": draw_slot_position(jax.random.fold_in(jax.random.fold_in(splits[5], part), 71), part),
        "context_lengths": draw_context_lengths(jax.random.fold_in(jax.random.fold_in(splits[5], part), 71), part),
        "value_up": normal_values(splits[4], (H, DL, VH), 0.35, 2.09375, ((0, 16),)),
    }


softmax_scale = 192.0 ** -0.5
masked_score = -1.0e30


def request_output(request_item, value_up):
    query_rows, cache_rows, positions, length = request_item
    scores = jnp.dot(query_rows, cache_rows.T, preferred_element_type=jnp.float32) * softmax_scale
    usable = (positions < length)[None, :]
    row_peak = jnp.max(jnp.where(usable, scores, masked_score), axis=1, keepdims=True)
    weights = jnp.where(usable, jnp.exp(scores - row_peak), jnp.float32(0.0))
    row_total = jnp.sum(weights, axis=1, keepdims=True)
    mixed_sum = jnp.dot(weights.astype(jnp.bfloat16), cache_rows[:, :DL], preferred_element_type=jnp.float32)
    latent_out = (mixed_sum / row_total).astype(jnp.bfloat16)
    projected = jnp.einsum("hl,hlv->hv", latent_out.astype(jnp.float32), value_up.astype(jnp.float32))
    return projected.astype(jnp.bfloat16).reshape(H * VH)


def reference(absorbed_query, latent_cache, slot_position, context_lengths, value_up):
    def per_request(request_item):
        return request_output(request_item, value_up)

    return lax.map(per_request, (absorbed_query, latent_cache, slot_position, context_lengths))
```

```python
import functools
import math

import jax
import jax.numpy as jnp
from jax import lax
from jax.experimental import pallas as pl
from jax.experimental.pallas import tpu as pltpu
from jax.sharding import PartitionSpec as P

softmax_scale = 192.0 ** (-0.5)
LOG2E = math.log2(math.e)
masked_score = -1e30
MESH = pl.DeviceIdType.MESH
LANES = 128


def packed(mixed, lse):
    lanes = lax.broadcasted_iota(jnp.int32, (mixed.shape[0], LANES), 1)
    high = lse.astype(jnp.bfloat16).astype(jnp.float32)
    rest = lse - high
    middle = rest.astype(jnp.bfloat16).astype(jnp.float32)
    low = rest - middle
    return mixed.astype(jnp.bfloat16), jnp.where(
        lanes == 0, high, jnp.where(lanes == 1, middle, low)
    ).astype(jnp.bfloat16)


def unpacked(ref, latent):
    mixed = ref[:, :latent].astype(jnp.float32)
    tail = ref[:, latent:].astype(jnp.float32)
    return mixed, (tail[:, 0:1] + tail[:, 1:2]) + tail[:, 2:3]


def kernel(
    chips, q_hbm, k_hbm, pos_hbm, len_hbm, w_hbm, out_ref,
    kbuf, wbuf, pos_ref, len_ref, qall, qrows, keep, keep_lse,
    send1, recv1, send2, recv2, lse_out, lse_in, final,
    k_sem, w_sem, pos_sem, len_sem, own_sem,
    q_send, q_recv, relay_send, relay_recv,
    half_send, half_recv, part_send, part_recv, lse_send, lse_recv,
):
    requests, heads_here, width = q_hbm.shape
    slots = kbuf.shape[2]
    latent = wbuf.shape[1]
    half = chips * heads_here
    me = lax.axis_index("kv")
    core, chip = lax.rem(me, 2), me // 2
    partner = {"kv": chip * 2 + 1 - core}
    others = []
    for i in range(chips - 1):
        there = i + (chip <= i).astype(jnp.int32)
        others.append((there, {"kv": there * 2 + core}))

    def remote(src, dst, send_sem, recv_sem, peer):
        pltpu.make_async_remote_copy(
            src_ref=src, dst_ref=dst, send_sem=send_sem, recv_sem=recv_sem,
            device_id=peer, device_id_type=MESH,
        ).start()

    def landed(ref, sem):
        pltpu.make_async_copy(ref, ref, sem).wait()

    barrier = pltpu.get_barrier_semaphore()
    for peer in [partner] + [peer for _, peer in others]:
        pl.semaphore_signal(barrier, inc=1, device_id=peer, device_id_type=MESH)
    for r in range(requests):
        pltpu.make_async_copy(q_hbm.at[r], qall.at[r, 0, chip], own_sem.at[r]).start()
    pltpu.make_async_copy(pos_hbm, pos_ref, pos_sem).start()
    pltpu.make_async_copy(len_hbm, len_ref, len_sem).start()
    pl.semaphore_wait(barrier, chips)

    for r in range(requests):
        for _, peer in others:
            remote(q_hbm.at[r], qall.at[r, 0, chip], q_send, q_recv.at[r], peer)
    for r in range(requests):
        pltpu.make_async_copy(k_hbm.at[r], kbuf.at[r], k_sem.at[r]).start()
    pltpu.make_async_copy(w_hbm, wbuf, w_sem).start()
    landed(pos_ref, pos_sem)
    pltpu.make_async_copy(len_hbm, len_ref, len_sem).wait()

    def relay(r):
        landed(qall.at[r, 0, chip], own_sem.at[r])
        landed(qall.at[r, 0, pl.ds(0, chips - 1)], q_recv.at[r])
        remote(qall.at[r, 0], qall.at[r, 1], relay_send, relay_recv.at[r], partner)

    def attend(r):
        landed(qall.at[r, 1], relay_recv.at[r])
        if heads_here % 8 == 0:
            queries = qall[r].astype(jnp.float32).reshape(2 * half, width)
        else:
            for c in range(2):
                for place in range(chips):
                    first = c * half + place * heads_here
                    qrows[first : first + heads_here, :] = qall[r, c, place].astype(jnp.float32)
            queries = qrows[...]
        queries = queries.astype(jnp.bfloat16)
        pltpu.make_async_copy(k_hbm.at[r], kbuf.at[r], k_sem.at[r]).wait()
        cut = slots // 2
        if cut % LANES:
            spans = [(0, slots)]
        else:
            spans = [(0, cut), (cut, slots)]

        def scored(span):
            scores = lax.dot_general(
                queries, kbuf[r, :, span[0] : span[1]],
                (((1,), (0,)), ((), ())), preferred_element_type=jnp.float32,
            )
            usable = pos_ref[r : r + 1, span[0] : span[1]] < len_ref[r]
            return jnp.where(usable, scores, masked_score)

        parts = []
        coming = scored(spans[0])
        for n, span in enumerate(spans):
            scores = coming
            if n + 1 < len(spans):
                coming = scored(spans[n + 1])
            peak = jnp.max(scores, axis=1, keepdims=True)
            weights = jnp.exp2((scores - peak) * (softmax_scale * LOG2E))
            total = jnp.sum(weights, axis=1, keepdims=True)
            mixed = lax.dot_general(
                weights.astype(jnp.bfloat16), kbuf[r, :latent, span[0] : span[1]],
                (((1,), (1,)), ((), ())), preferred_element_type=jnp.float32,
            )
            parts.append((mixed, peak, total))
        peak = functools.reduce(jnp.maximum, [p for _, p, _ in parts])
        factors = [jnp.exp2((p - peak) * (softmax_scale * LOG2E)) for _, p, _ in parts]
        total = sum(f * t for f, (_, _, t) in zip(factors, parts))
        inverse = 1.0 / total
        mixed = sum(m * (f * inverse) for f, (m, _, _) in zip(factors, parts))
        return mixed, peak * softmax_scale + jnp.log(total)

    def reduce1(r):
        mixed, lse = attend(r)
        values, tail = packed(mixed[half:], lse[half:])
        send1[r, :, :latent] = values
        send1[r, :, latent:] = tail
        remote(send1.at[r], recv1.at[r], half_send, half_recv.at[r], partner)
        keep[r] = mixed[:half]
        keep_lse[r] = jnp.broadcast_to(lse[:half], (half, LANES))

    def reduce2(r):
        landed(recv1.at[r], half_recv.at[r])
        there, there_lse = unpacked(recv1.at[r], latent)
        here_lse = keep_lse[r, :, 0:1]
        peak = jnp.maximum(here_lse, there_lse)
        here_factor, there_factor = jnp.exp(here_lse - peak), jnp.exp(there_lse - peak)
        total = here_factor + there_factor
        inverse = 1.0 / total
        mixed = keep[r] * (here_factor * inverse) + there * (there_factor * inverse)
        lse = peak + jnp.log(total)
        diagonal = lax.broadcasted_iota(jnp.int32, (half, LANES), 0) == lax.broadcasted_iota(
            jnp.int32, (half, LANES), 1
        )
        row = jnp.sum(jnp.where(diagonal, lse, 0.0), axis=0, keepdims=True)
        lse_out[r] = row
        for place in range(chips):
            send2[r, place] = mixed[place * heads_here : (place + 1) * heads_here].astype(jnp.bfloat16)
        for place, peer in others:
            remote(send2.at[r, place], recv2.at[r, chip], part_send, part_recv.at[r], peer)
            remote(lse_out.at[r], lse_in.at[r, chip], lse_send, lse_recv.at[r], peer)
        recv2[r, chip] = send2[r, chip]
        lse_in[r, chip] = row

    def reduce3(r):
        landed(lse_in.at[r, pl.ds(0, chips - 1)], lse_recv.at[r])
        rows = [lse_in[r, place] for place in range(chips)]
        peak = functools.reduce(jnp.maximum, rows)
        factors = [jnp.exp(row - peak) for row in rows]
        inverse = 1.0 / sum(factors[1:], factors[0])
        mine = lax.broadcasted_iota(jnp.int32, (heads_here, LANES), 1) == (
            lax.broadcasted_iota(jnp.int32, (heads_here, LANES), 0) + chip * heads_here
        )
        shares = [
            jnp.sum(jnp.where(mine, f * inverse, 0.0), axis=1, keepdims=True) for f in factors
        ]
        landed(recv2.at[r, pl.ds(0, chips - 1)], part_recv.at[r])
        mixed = recv2[r, 0].astype(jnp.float32) * shares[0]
        for place in range(1, chips):
            mixed = mixed + recv2[r, place].astype(jnp.float32) * shares[place]
        final[r] = mixed

    for r in range(min(2, requests)):
        relay(r)
    for r in range(requests):
        reduce1(r)
        if r + 2 < requests:
            relay(r + 2)
        if r:
            reduce2(r - 1)
    reduce2(requests - 1)
    landed(qall.at[:, 0, pl.ds(0, chips - 1)], q_send)
    landed(qall.at[:, 0], relay_send)
    landed(send1, half_send)
    pltpu.make_async_copy(w_hbm, wbuf, w_sem).wait()
    for r in range(requests):
        reduce3(r)
    value = wbuf.shape[2]
    for h in range(heads_here):
        rows = final[:, h, :].astype(jnp.bfloat16)
        out_ref[:, h * value : (h + 1) * value] = jnp.dot(
            rows, wbuf[h], preferred_element_type=jnp.float32
        ).astype(out_ref.dtype)
    landed(recv2.at[:, pl.ds(0, chips - 1)], part_send)
    landed(lse_in.at[:, pl.ds(0, chips - 1)], lse_send)


def shards(devices, absorbed_query, latent_cache, slot_position, context_lengths, value_up):
    chips = devices // 2
    requests, heads_here, width = absorbed_query.shape
    slots = latent_cache.shape[1]
    latent, value = value_up.shape[1:]
    heads = devices * heads_here
    wide = latent + LANES
    half = heads // 2
    hbm = pl.BlockSpec(memory_space=pltpu.HBM)
    bf16, f32 = jnp.bfloat16, jnp.float32
    dma = pltpu.SemaphoreType.DMA
    each = dma((requests,))
    return pl.pallas_call(
        functools.partial(kernel, chips),
        out_shape=pltpu.VMEM((requests, heads_here * value), bf16),
        in_specs=[hbm] * 5,
        out_specs=pl.BlockSpec(memory_space=pltpu.VMEM),
        scratch_shapes=[
            pltpu.VMEM((requests, width, slots), bf16),
            pltpu.VMEM(value_up.shape, bf16),
            pltpu.VMEM(slot_position.shape, jnp.int32),
            pltpu.SMEM(context_lengths.shape, jnp.int32),
            pltpu.VMEM((requests, 2, chips, heads_here, width), bf16),
            pltpu.VMEM((heads if heads_here % 8 else 8, width), f32),
            pltpu.VMEM((requests, half, latent), f32),
            pltpu.VMEM((requests, half, LANES), f32),
            pltpu.VMEM((requests, half, wide), bf16),
            pltpu.VMEM((requests, half, wide), bf16),
            pltpu.VMEM((requests, chips, heads_here, latent), bf16),
            pltpu.VMEM((requests, chips, heads_here, latent), bf16),
            pltpu.VMEM((requests, 1, LANES), f32),
            pltpu.VMEM((requests, chips, 1, LANES), f32),
            pltpu.VMEM((requests, heads_here, latent), f32),
            each, dma, dma, dma, each,
            dma, each, dma, each,
            dma, each, dma, each, dma, each,
        ],
        compiler_params=pltpu.CompilerParams(
            collective_id=0, has_side_effects=True, vmem_limit_bytes=56 * 1024 * 1024
        ),
        name="attention_step",
    )(absorbed_query, jnp.swapaxes(latent_cache, 1, 2), slot_position, context_lengths, value_up)


def solution(mesh):
    return jax.shard_map(
        functools.partial(shards, mesh.shape["kv"]),
        mesh=mesh,
        in_specs=(
            P("grp", "kv", None),
            P("grp", "kv", None),
            P("grp", "kv"),
            P("grp"),
            P("kv", None, None),
        ),
        out_specs=P("grp", "kv"),
        check_vma=False,
    )
```
